256 devices in a mesh: pipe: 4 (over y_hi, core), section: 8 (over y_lo, x), tp: 8 (over z).
Axes of the slice: x: 4, y: 4 (y_hi: 2, y_lo: 2; y = y_hi * 2 + y_lo), z: 8, core: 2. Of those that a mesh axis runs over, the one named last changes fastest.
Arguments:
- weights: bfloat16 [4, 8, 2, 4096, 512], P('pipe', 'section', None, 'tp'), may hold values from -6 to 6
- first_moment: float32 [4, 8, 2, 4096, 512], P('pipe', 'section', None, 'tp'), may hold values from -4 to 4
- second_moment: float32 [4, 8, 2, 4096, 512], P('pipe', 'section', None, 'tp'), may hold values from 0.1 to 2
- gradients: bfloat16 [4, 8, 2, 4096, 512], P('pipe', 'section', None, 'tp'), may hold values from -6 to 6
- old_section: int32 [4, 12], replicated, may hold values from 0 to 7, as said below
- new_section: int32 [12], replicated, may hold values from 0 to 7, as said below
- lost_pipe: int32 [4], replicated, may hold values from 0 to 3, each once
- donor_offset: int32 [12], replicated, may hold values from 1 to 3
Outputs:
- new_weights: bfloat16 [4, 8, 2, 4096, 512], P('pipe', 'section', None, 'tp')
- new_first: float32 [4, 8, 2, 4096, 512], P('pipe', 'section', None, 'tp')
- new_second: float32 [4, 8, 2, 4096, 512], P('pipe', 'section', None, 'tp')
The draws below stay inside these ranges and needn't reach their ends.
Inputs may be any that keep to these rules, and one draw needn't show every extreme that they name: `old_section`: each row places layers in section order (a layer's section never falls with the layer); 4 sections of each row hold exactly 2 layers and the others one each. `new_section`: layers in any order; no section holds more than 2 layers, and some section holds exactly 2.
All inputs are finite; a program needn't handle non-finite values.
Results may differ from the reference program's by a relative error of at most 0.0075.
Values may be sent and summed in bfloat16 or wider, within the bound.
A program may use at most 64 MiB of HBM per device.

```python
import math
import jax
import jax.numpy as jnp
from jax import lax

ROWS = 4096
KV_COLS = 512
CAP = 2
PIPES = 4
SECTIONS = 8
LAYERS = 12


def section_rows(key, doubles, singles):
    order = jax.random.permutation(key, SECTIONS)
    ranking = jnp.argsort(order).astype(jnp.int32)
    counts = jnp.where(ranking < doubles, 2, jnp.where(ranking < doubles + singles, 1, 0)).astype(jnp.int32)
    ending = jnp.cumsum(counts).astype(jnp.int32)
    layer_ids = jnp.arange(LAYERS, dtype=jnp.int32)
    return jnp.sum((ending[None, :] <= layer_ids[:, None]).astype(jnp.int32), axis=1).astype(jnp.int32)


def draw_old_section(key, part):
    base = jax.random.fold_in(key, 11)
    row_keys = jax.random.split(base, PIPES)
    return jax.vmap(lambda row_key: section_rows(row_key, SECTIONS // 2, SECTIONS // 2))(row_keys)


def draw_new_section(key, part):
    base = jax.random.fold_in(key, 23)
    slots = jax.random.permutation(base, SECTIONS * CAP).astype(jnp.int32)
    return (slots[:LAYERS] // CAP).astype(jnp.int32)


def touch_ends(result, own_key, low, top_value):
    longest = result.shape.index(max(result.shape))
    spots = []
    for shift in (0, 1):
        where = [jax.random.randint(jax.random.fold_in(own_key, axis), (), 0, length) for axis, length in enumerate(result.shape)]
        where[longest] = (where[longest] + shift) % result.shape[longest]
        spots.append(tuple(where))
    return result.at[spots[0]].set(low).at[spots[1]].set(top_value)


def block_levels(key, shape, cuts, least, top_value):
    gain, own = 1.0, jax.random.fold_in(key, 6)
    for axis_at, shards_of in cuts:
        heights = jnp.exp(jax.random.uniform(jax.random.fold_in(own, axis_at), (shards_of,), jnp.float32, least / len(cuts), top_value / len(cuts)))
        gain = gain * jnp.repeat(heights, shape[axis_at] // shards_of).reshape([-1 if axis == axis_at else 1 for axis in range(len(shape))])
    return gain


def scatter_about(stream_key, extent, spread, bound, shards=(), kind=jnp.bfloat16):
    result = spread * jax.random.normal(stream_key, extent, jnp.float32)
    if shards:
        result = result * block_levels(stream_key, extent, shards, -0.22, 0.18)
    return jnp.clip(result, -bound, bound).astype(kind)


def setup_inputs(seed: int = 0) -> dict:
    streams_of = jax.random.split(jax.random.key(seed), 9)
    return {
        "weights": scatter_about(streams_of[0], (PIPES, SECTIONS, CAP, ROWS, KV_COLS), 1.0, 6.0, ((0, 4), (1, 8), (3, 8))),
        "first_moment": scatter_about(streams_of[1], (PIPES, SECTIONS, CAP, ROWS, KV_COLS), 0.5, 4.0, ((0, 4), (1, 8), (3, 8)), jnp.float32),
        "second_moment": jnp.clip(jnp.exp(math.log(2.0) - 2.9957323 * jax.random.uniform(streams_of[2], (PIPES, SECTIONS, CAP, ROWS, KV_COLS), jnp.float32) ** block_levels(streams_of[2], (PIPES, SECTIONS, CAP, ROWS, KV_COLS), ((0, 4), (1, 8), (3, 8)), -0.2, 0.2)), 0.1, 2.0),
        "gradients": scatter_about(streams_of[3], (PIPES, SECTIONS, CAP, ROWS, KV_COLS), 1.0, 6.0, ((0, 4), (1, 8), (3, 8))),
        "old_section": draw_old_section(jax.random.fold_in(streams_of[8], 71), 0),
        "new_section": draw_new_section(jax.random.fold_in(streams_of[8], 71), 0),
        "lost_pipe": jax.random.permutation(streams_of[6], PIPES).astype(jnp.int32),
        "donor_offset": touch_ends(jax.random.randint(streams_of[7], (LAYERS,), 1, PIPES), jax.random.fold_in(streams_of[7], 1), 1, PIPES - 1).astype(jnp.int32),
    }


LEARN_RATE = 0.01
BETA_ONE = 0.9
BETA_TWO = 0.95
EPSILON = 1e-08
DECAY_RATE = 0.1

def slot_ranks(section_map):
    layer_ids = jnp.arange(section_map.shape[-1], dtype=jnp.int32)
    same_section = section_map[..., :, None] == section_map[..., None, :]
    before = layer_ids[None, :] < layer_ids[:, None]
    return lax.optimization_barrier(jnp.sum((same_section & before).astype(jnp.int32), axis=-1)).astype(jnp.int32)

def reference(weights, first_moment, second_moment, gradients, old_section, new_section, lost_pipe, donor_offset):
    pipe_ids = jnp.arange(PIPES, dtype=jnp.int32)
    layer_ids = jnp.arange(LAYERS, dtype=jnp.int32)
    is_lost = pipe_ids == lost_pipe[0]
    now_section = jnp.where(is_lost[:, None], new_section[None, :], old_section).astype(jnp.int32)
    now_slot = slot_ranks(now_section)
    old_slot = slot_ranks(old_section)
    donors = lost_pipe[donor_offset].astype(jnp.int32)
    source = jnp.where(is_lost[:, None], donors[None, :], pipe_ids[:, None]).astype(jnp.int32)
    source_section = old_section[source, layer_ids[None, :]]
    source_slot = old_slot[source, layer_ids[None, :]]
    grad_rows = gradients[pipe_ids[:, None], now_section, now_slot].astype(jnp.float32)
    mean_grad = lax.optimization_barrier(jnp.sum(grad_rows, axis=0)) / PIPES
    weight_now = weights[source, source_section, source_slot].astype(jnp.float32)
    moment_one = first_moment[source, source_section, source_slot]
    moment_two = second_moment[source, source_section, source_slot]
    next_one = BETA_ONE * moment_one + (1.0 - BETA_ONE) * mean_grad[None]
    next_two = BETA_TWO * moment_two + (1.0 - BETA_TWO) * mean_grad[None] * mean_grad[None]
    update = next_one / (jnp.sqrt(next_two) + EPSILON) + DECAY_RATE * weight_now
    next_weight = (weight_now - LEARN_RATE * update).astype(jnp.bfloat16)
    out_weight = jnp.zeros(weights.shape, jnp.bfloat16).at[pipe_ids[:, None], now_section, now_slot].set(next_weight)
    out_one = jnp.zeros(first_moment.shape, jnp.float32).at[pipe_ids[:, None], now_section, now_slot].set(next_one)
    out_two = jnp.zeros(second_moment.shape, jnp.float32).at[pipe_ids[:, None], now_section, now_slot].set(next_two)
    return (out_weight, out_one, out_two)
```

```python
import functools

import jax
import jax.numpy as jnp
from jax import lax
from jax.experimental import pallas as pl
from jax.experimental.pallas import tpu as pltpu
from jax.sharding import PartitionSpec as P

LEARN_RATE = 0.01
BETA_ONE = 0.9
BETA_TWO = 0.95
EPSILON = 1e-08
DECAY_RATE = 0.1
MESH = pl.DeviceIdType.MESH
LAYERS = 12
BAND = 16
COLS = 512

def section_layers(section):
    last = section + min(section + 1, 4)
    return list(range(section + max(0, section - 4), last + 1))


CANDIDATES = [sorted(set(section_layers(x) + section_layers(x + 4))) for x in range(4)]
HELD = len(CANDIDATES[0])


def pick(index, values):
    out = jnp.int32(values[0])
    for at in range(1, len(values)):
        out = jnp.where(index == at, jnp.int32(values[at]), out)
    return out


def exchange_kernel(
    g_hbm, w_hbm, one_hbm, two_hbm, old_ref, new_ref, lost_ref, donor_ref,
    out_a, out_two, out_w,
    one_f, two_f, one_b, two_b,
    s1_w, s1_one, s1_two, s2s_w, s2s_one, s2s_two, s2r_w, s2r_one, s2r_two,
    g1, g2s, g2r, mean,
    r1s_a, r1s_two, r1s_w, r1r_a, r1r_two, r1r_w,
    r2s_a, v_a, v_two, v_w,
    t_pick, t_src, t_grad, t_lost, t_red, t_new, t_unit,
    send_sem, recv_sem, local_sem,
):
    pipe = lax.axis_index("pipe")
    section = lax.axis_index("section")
    tp = lax.axis_index("tp")
    y = (pipe // 2) * 2 + section // 4
    x = section % 4
    c = pipe % 2

    def device(yy, xx, cc):
        return ((yy // 2) * 2 + cc, (yy % 2) * 4 + xx, tp)

    counters = {"remote": 0, "local": 0}

    def remote(src, dst, target):
        at = counters["remote"]
        counters["remote"] = at + 1
        copy = pltpu.make_async_remote_copy(
            src_ref=src, dst_ref=dst, send_sem=send_sem.at[at], recv_sem=recv_sem.at[at],
            device_id=target, device_id_type=MESH,
        )
        copy.start()
        return copy

    def local(src, dst):
        at = counters["local"]
        counters["local"] = at + 1
        copy = pltpu.make_async_copy(src, dst, local_sem.at[at])
        copy.start()
        return copy

    def wait(copies):
        for copy in copies:
            copy.wait()

    x_core = [(dx, dc) for dx in (1, 3, 2) for dc in (0, 1)] + [(0, 1)]
    y_core = [(dy, dc) for dy in (1, 3, 2) for dc in (0, 1)] + [(0, 1)]

    load_one = local(one_hbm, one_f)
    load_two = local(two_hbm, two_f)

    barrier = pltpu.get_barrier_semaphore()
    greeted = [((y, (x + dx) % 4, (c + dc) % 2)) for dx, dc in x_core]
    greeted += [(((y + dy) % 4, x, (c + dc) % 2)) for dy, dc in y_core[:-1]]
    for yy, xx, cc in greeted:
        pl.semaphore_signal(barrier, inc=1, device_id=device(yy, xx, cc), device_id_type=MESH)
    pl.semaphore_wait(barrier, len(greeted))

    me_y = (y * 2 + c) * 2
    me_x = (x * 2 + c) * 2
    grad_one = []
    for dy, dc in y_core:
        yy, cc = (y + dy) % 4, (c + dc) % 2
        grad_one.append(remote(g_hbm.at[:, :, cc, yy], g1.at[pl.ds(me_y, 2)], device(yy, x, cc)))
    grad_one.append(local(g_hbm.at[:, :, c, y], g1.at[pl.ds(me_y, 2)]))

    def state_first(src, dst):
        copies = []
        for dx, dc in x_core:
            xx, cc = (x + dx) % 4, (c + dc) % 2
            copies.append(remote(src.at[:, xx * 2 + cc], dst.at[pl.ds(me_x, 2)], device(y, xx, cc)))
        copies.append(local(src.at[:, x * 2 + c], dst.at[pl.ds(me_x, 2)]))
        return copies

    first_w = state_first(w_hbm, s1_w)

    def narrow(src, dst):
        def body(at, carry):
            dst[at // 8, at % 8] = src[at // 8, at % 8].astype(jnp.bfloat16)
            return carry

        lax.fori_loop(0, 16, body, 0)

    load_one.wait()
    narrow(one_f, one_b)
    first_one = state_first(one_b, s1_one)
    load_two.wait()
    narrow(two_f, two_b)

    lost = lost_ref[0]
    lost_half, lost_core = lost // 2, lost % 2
    row = y % 2
    for j in range(8):
        layer = 4 * row + j
        donor = lost_ref[donor_ref[layer]]
        there = old_ref[donor, layer]
        twin = old_ref[donor, jnp.maximum(layer - 1, 0)]
        slot = jnp.where((layer > 0) & (twin == there), 1, 0)
        t_pick[j] = ((there % 4) * 2 + donor % 2) * 2 + slot
    for layer in range(LAYERS):
        donor = lost_ref[donor_ref[layer]]
        there = old_ref[donor, layer]
        t_src[layer] = ((donor // 2) * 2 + there // 4) * 8 + layer - 4 * (there // 4)
    for k in range(HELD):
        layer = pick(x, [CANDIDATES[at][k] for at in range(4)])
        for relay in range(4):
            there = old_ref[relay, layer]
            twin = old_ref[relay, jnp.maximum(layer - 1, 0)]
            slot = jnp.where((layer > 0) & (twin == there), 1, 0)
            held = (there % 4 == x) & (lost != relay)
            from_y = (relay // 2) * 2 + there // 4
            t_grad[k * 4 + relay] = jnp.where(held, (from_y * 2 + relay % 2) * 2 + slot, 16)
    for e in range(4):
        t_lost[e] = ((lost_half * 2 + e // 2) * 2 + lost_core) * 2 + e % 2
    new_at = [new_ref[layer] for layer in range(LAYERS)]
    inverse = [jnp.int32(0)] * 16
    for layer in range(LAYERS):
        there = new_at[layer]
        slot = jnp.int32(0)
        for before in range(layer):
            slot = slot + jnp.where(new_at[before] == there, 1, 0)
        t_red[layer] = (there % 4) * (HELD + 4) + HELD + (there // 4) * 2 + slot
        place = there * 2 + slot
        inverse = [jnp.where(place == at, layer, inverse[at]) for at in range(16)]
    for xx in range(4):
        for e in range(4):
            t_new[xx * 4 + e] = inverse[((e // 2) * 4 + xx) * 2 + e % 2]
    held_at = [pick(x, [CANDIDATES[at][k] for at in range(4)]) for k in range(HELD)]
    entries = {}
    for relay in range(4):
        for r in range(2):
            first = jnp.int32(0)
            for layer in range(LAYERS):
                first = first + jnp.where(old_ref[relay, layer] < r * 4 + x, 1, 0)
            for slot in range(2):
                position = jnp.int32(0)
                for k in range(HELD):
                    position = position + jnp.where(held_at[k] < first + slot, 1, 0)
                entries[relay, r, slot] = jnp.minimum(position, HELD - 1)
    for yy in range(4):
        half, r = yy // 2, yy % 2
        here = lost_half == half
        for slot in range(2):
            even, odd = entries[half * 2, r, slot], entries[half * 2 + 1, r, slot]
            t_unit[yy * 4 + slot] = jnp.where(here & (lost_core == 0), odd, even)
            t_unit[yy * 4 + 2 + slot] = jnp.where(here, HELD + r * 2 + slot, odd)

    g1[16] = jnp.zeros((4, BAND, COLS), jnp.bfloat16)
    wait(grad_one)

    def grad_merge(k, carry):
        total = g1[t_grad[k * 4]].astype(jnp.float32)
        for relay in range(1, 4):
            total = total + g1[t_grad[k * 4 + relay]].astype(jnp.float32)
        g2s[:, k] = total.astype(jnp.bfloat16)
        return carry

    lax.fori_loop(0, HELD, grad_merge, 0)

    def grad_lost(e, carry):
        g2s[:, HELD + e] = g1[t_lost[e]]
        return carry

    lax.fori_loop(0, 4, grad_lost, 0)

    def x_exchange(src, dst):
        copies = []
        for dx in (1, 3, 2):
            xx = (x + dx) % 4
            copies.append(remote(src.at[xx], dst.at[x], device(y, xx, c)))
        copies.append(local(src.at[x], dst.at[x]))
        return copies

    def y_exchange(src, dst):
        copies = []
        for dy in (1, 3, 2):
            yy = (y + dy) % 4
            copies.append(remote(src.at[yy], dst.at[y], device(yy, x, c)))
        copies.append(local(src.at[y], dst.at[y]))
        return copies

    grad_two = x_exchange(g2s, g2r)

    def state_second(src, send, dst):
        def body(j, carry):
            send[:, j] = src[t_pick[j]]
            return carry

        lax.fori_loop(0, 8, body, 0)
        return y_exchange(send, dst)

    wait(first_w)
    second_w = state_second(s1_w, s2s_w, s2r_w)

    def state_at(ref, layer):
        at = t_src[layer]
        return ref[at // 8, at % 8]

    wait(second_w)

    def pack_w(i, carry):
        r1s_w[i // 4, i % 4] = state_at(s2r_w, t_new[i])
        return carry

    lax.fori_loop(0, 16, pack_w, 0)
    back_w = x_exchange(r1s_w, r1r_w)
    first_two = state_first(two_b, s1_two)

    wait(first_one)
    second_one = state_second(s1_one, s2s_one, s2r_one)

    wait(grad_two)
    for layer in range(LAYERS):
        at = t_red[layer]
        total = g2r[at // (HELD + 4), at % (HELD + 4)].astype(jnp.float32)
        for xx in range(4):
            if layer in CANDIDATES[xx]:
                total = total + g2r[xx, CANDIDATES[xx].index(layer)].astype(jnp.float32)
        mean[layer] = total * 0.25
    for xx in range(4):
        for k in range(HELD):
            r1s_a[xx, k] = mean[CANDIDATES[xx][k]].astype(jnp.bfloat16)

    wait(second_one)

    def pack_one(i, carry):
        layer = t_new[i]
        value = BETA_ONE * state_at(s2r_one, layer).astype(jnp.float32) + (1.0 - BETA_ONE) * mean[layer]
        r1s_a[i // 4, HELD + i % 4] = value.astype(jnp.bfloat16)
        return carry

    lax.fori_loop(0, 16, pack_one, 0)
    back_a = x_exchange(r1s_a, r1r_a)

    def y_return(src_of, dst):
        copies = []
        for dy in (1, 3, 2):
            yy = (y + dy) % 4
            copies.append(remote(src_of(yy), dst.at[:, y], device(yy, x, c)))
        copies.append(local(src_of(y), dst.at[:, y]))
        return copies

    wait(back_w)
    down_w = y_return(lambda yy: r1r_w.at[:, pl.ds((yy % 2) * 2, 2)], v_w)

    wait(first_two)
    second_two = state_second(s1_two, s2s_two, s2r_two)

    wait(back_a)

    def pack_units(i, carry):
        r2s_a[i // 4, :, i % 4] = r1r_a[:, t_unit[i]]
        return carry

    lax.fori_loop(0, 16, pack_units, 0)
    down_a = y_return(lambda yy: r2s_a.at[yy], v_a)

    wait(second_two)

    def pack_two(i, carry):
        layer = t_new[i]
        grad = mean[layer]
        value = BETA_TWO * state_at(s2r_two, layer).astype(jnp.float32) + (1.0 - BETA_TWO) * grad * grad
        r1s_two[i // 4, i % 4] = value.astype(jnp.bfloat16)
        return carry

    lax.fori_loop(0, 16, pack_two, 0)
    back_two = x_exchange(r1s_two, r1r_two)

    def core_swap(src, dst):
        return [remote(src, dst.at[:, c], device(y, x, 1 - c)), local(src, dst.at[:, c])]

    wait(down_w)
    swaps = core_swap(v_w, out_w)
    wait(back_two)
    down_two = y_return(lambda yy: r1r_two.at[:, pl.ds((yy % 2) * 2, 2)], v_two)
    wait(down_a)
    swaps += core_swap(v_a, out_a)
    wait(down_two)
    swaps += core_swap(v_two, out_two)
    wait(swaps)


def exchange(grads, weights, one, two, old_section, new_section, lost_pipe, donor_offset):
    bf16, f32, i32 = jnp.bfloat16, jnp.float32, jnp.int32
    any_space = pl.BlockSpec(memory_space=pl.ANY)
    smem = pl.BlockSpec(memory_space=pltpu.SMEM)
    vm = lambda shape, dtype=bf16: pltpu.VMEM(shape + (BAND, COLS), dtype)
    state = (2, 8, 4)
    return pl.pallas_call(
        exchange_kernel,
        out_shape=(
            jax.ShapeDtypeStruct((4, 2, 4, 4, BAND, COLS), bf16),
            jax.ShapeDtypeStruct((4, 2, 4, 2, BAND, COLS), bf16),
            jax.ShapeDtypeStruct((4, 2, 4, 2, BAND, COLS), bf16),
        ),
        in_specs=[any_space] * 4 + [smem] * 4,
        out_specs=(any_space, any_space, any_space),
        scratch_shapes=[
            vm(state, f32), vm(state, f32), vm(state), vm(state),
            vm((16, 4)), vm((16, 4)), vm((16, 4)),
            vm((4, 8)), vm((4, 8)), vm((4, 8)),
            vm((4, 8)), vm((4, 8)), vm((4, 8)),
            vm((17, 4)), vm((4, HELD + 4)), vm((4, HELD + 4)), vm((LAYERS,), f32),
            vm((4, HELD + 4)), vm((4, 4)), vm((4, 4)),
            vm((4, HELD + 4)), vm((4, 4)), vm((4, 4)),
            vm((4, 4, 4)), vm((4, 4, 4)), vm((4, 4, 2)), vm((4, 4, 2)),
            pltpu.SMEM((8,), i32), pltpu.SMEM((LAYERS,), i32), pltpu.SMEM((HELD * 4,), i32), pltpu.SMEM((4,), i32),
            pltpu.SMEM((LAYERS,), i32), pltpu.SMEM((16,), i32), pltpu.SMEM((16,), i32),
            pltpu.SemaphoreType.DMA((64,)), pltpu.SemaphoreType.DMA((64,)), pltpu.SemaphoreType.DMA((32,)),
        ],
        compiler_params=pltpu.CompilerParams(collective_id=0, has_side_effects=True, vmem_limit_bytes=48 << 20),
        name="exchange",
    )(
        grads.reshape(2, 4, 2, 4, BAND, COLS),
        weights.reshape(2, 8, 4, BAND, COLS),
        one.reshape(2, 8, 4, BAND, COLS),
        two.reshape(2, 8, 4, BAND, COLS),
        old_section, new_section, lost_pipe, donor_offset,
    )


def adam_kernel(info, a_ref, two_in, w_in, w_ref, one_ref, two_ref, out_w, out_one, out_two):
    slot = pl.program_id(0)
    rows = out_w.shape[1]
    keep = slot < info[2]

    def finish(weight, next_one, next_two):
        update = next_one / (jnp.sqrt(next_two) + EPSILON) + DECAY_RATE * weight
        next_weight = weight - LEARN_RATE * update
        out_w[0] = jnp.where(keep, next_weight, 0.0).astype(jnp.bfloat16)
        out_one[0] = jnp.where(keep, next_one, 0.0)
        out_two[0] = jnp.where(keep, next_two, 0.0)

    def wide(ref):
        return ref[...].astype(jnp.float32).reshape(rows, COLS)

    @pl.when(info[0] == 1)
    def _():
        finish(wide(w_in), wide(a_ref), wide(two_in))

    @pl.when(info[0] == 0)
    def _():
        grad = wide(a_ref)
        next_one = BETA_ONE * one_ref[0] + (1.0 - BETA_ONE) * grad
        next_two = BETA_TWO * two_ref[0] + (1.0 - BETA_TWO) * grad * grad
        finish(w_ref[0].astype(jnp.float32), next_one, next_two)


def adam(info, units, lost_two, lost_w, weights, one, two):
    chunk = 128
    moved = lambda at: pl.BlockSpec((1, 2, 4, 1, BAND, COLS), at)
    own = pl.BlockSpec(
        (1, chunk, COLS), lambda s, i, info: (jnp.where(info[0] == 1, 0, s), jnp.where(info[0] == 1, 0, i), 0)
    )
    lost_only = moved(
        lambda s, i, info: (jnp.where(info[0] == 1, i, 0), 0, 0, jnp.where(info[0] == 1, s, 0), 0, 0)
    )
    out = pl.BlockSpec((1, chunk, COLS), lambda s, i, info: (s, i, 0))
    return pl.pallas_call(
        adam_kernel,
        out_shape=(
            jax.ShapeDtypeStruct(weights.shape, jnp.bfloat16),
            jax.ShapeDtypeStruct(one.shape, jnp.float32),
            jax.ShapeDtypeStruct(two.shape, jnp.float32),
        ),
        grid_spec=pltpu.PrefetchScalarGridSpec(
            num_scalar_prefetch=1,
            grid=(2, 4),
            in_specs=[
                moved(lambda s, i, info: (i, 0, 0, info[1] + s, 0, 0)),
                lost_only, lost_only, own, own, own,
            ],
            out_specs=(out, out, out),
        ),
        compiler_params=pltpu.CompilerParams(dimension_semantics=("arbitrary", "arbitrary")),
        name="adam",
    )(info, units, lost_two, lost_w, weights, one, two)


def per_device(weights, first_moment, second_moment, gradients, old_section, new_section, lost_pipe, donor_offset):
    pipe, section = lax.axis_index("pipe"), lax.axis_index("section")
    weights, one, two, grads = weights[0, 0], first_moment[0, 0], second_moment[0, 0], gradients[0, 0]
    lost = lost_pipe[0]
    is_lost = lost == pipe
    own_map = jnp.where(is_lost, new_section, jnp.sum(jnp.where(jnp.arange(4)[:, None] == pipe, old_section, 0), axis=0))
    count = jnp.sum((own_map == section).astype(jnp.int32))
    base = jnp.where(is_lost, 2, jnp.where(lost // 2 == pipe // 2, 0, (pipe % 2) * 2))
    info = jnp.stack([is_lost.astype(jnp.int32), base.astype(jnp.int32), count])
    units, lost_two, lost_w = exchange(grads, weights, one, two, old_section, new_section, lost_pipe, donor_offset)
    out_w, out_one, out_two = adam(info, units, lost_two, lost_w, weights, one, two)
    return out_w[None, None], out_one[None, None], out_two[None, None]


def solution(mesh):
    big, small = P("pipe", "section", None, "tp", None), P()
    return jax.shard_map(
        per_device,
        mesh=mesh,
        in_specs=(big, big, big, big, small, small, small, small),
        out_specs=(big, big, big),
        check_vma=False,
    )
```

```python
from typing import Any, NamedTuple

import jax
import jax.numpy as jnp
from jax import lax
from jax.experimental import pallas as pl
from jax.experimental.pallas import tpu as pltpu
from jax.sharding import PartitionSpec as P

LEARN_RATE = 0.01
BETA_ONE = 0.9
BETA_TWO = 0.95
EPSILON = 1e-08
DECAY_RATE = 0.1
MESH = pl.DeviceIdType.MESH
LAYERS = 12
BAND = 16
COLS = 512

WEIGHT, FIRST, SECOND = range(3)
ALONG_X, ALONG_Y = range(2)
STREAMS = (
    (WEIGHT, ALONG_X, 0, 256),
    (WEIGHT, ALONG_X, 256, 256),
    (FIRST, ALONG_X, 0, 512),
    (SECOND, ALONG_Y, 0, 384),
    (SECOND, ALONG_Y, 384, 128),
)
W0, W1, ONE, TWO0, TWO1 = range(5)
S1, S2, R1, R2, R3, LOAD = range(6)
GRADS, MEANS, SMALL = range(10, 13)


def section_layers(section):
    last = section + min(section + 1, 4)
    return list(range(section + max(0, section - 4), last + 1))


CANDIDATES = [sorted(set(section_layers(x) + section_layers(x + 4))) for x in range(4)]
HELD = len(CANDIDATES[0])


class Buffers(NamedTuple):
    grads_in: Any
    state_in: Any
    maps_in: Any
    final: Any
    narrow: Any
    grad_one: Any
    grad_send: Any
    grad_two: Any
    mean: Any
    mean_send: Any
    mean_back: Any
    mean_down: Any
    pair_down: Any
    half_mean: Any
    half: Any
    units: Any
    lost_two: Any
    lost_w: Any
    one: Any
    two_send: Any
    two: Any
    back_send: Any
    back: Any
    maps: Any
    pick: Any
    src: Any
    grad_at: Any
    lost_at: Any
    sum_at: Any
    new_at: Any
    new_has: Any
    mean_at: Any
    unit_at: Any
    flags: Any
    sent: Any
    got: Any


def pick(index, values):
    out = jnp.int32(values[0])
    for at in range(1, len(values)):
        out = jnp.where(index == at, jnp.int32(values[at]), out)
    return out


def update(weight, next_one, next_two):
    change = next_one / (jnp.sqrt(next_two) + EPSILON) + DECAY_RATE * weight
    return weight - LEARN_RATE * change


def exchange_kernel(tree, *refs):
    ref = jax.tree.unflatten(tree, refs)
    pipe, section, tp = lax.axis_index("pipe"), lax.axis_index("section"), lax.axis_index("tp")
    y = (pipe // 2) * 2 + section // 4
    x = section % 4
    c = pipe % 2
    ring = (1, 3, 2)
    with_core = [(step, dc) for step in ring for dc in (0, 1)] + [(0, 1)]
    pending = {}

    def device(yy, xx, cc):
        return ((yy // 2) * 2 + cc, (yy % 2) * 4 + xx, tp)

    def begin(key, sends, own, landed, left):
        at = len(pending)
        assert at < ref.sent.shape[0]
        for src, dst, target in sends:
            pltpu.make_async_remote_copy(
                src_ref=src, dst_ref=dst, send_sem=ref.sent.at[at], recv_sem=ref.got.at[at],
                device_id=target, device_id_type=MESH,
            ).start()
        for src, dst in own:
            pltpu.make_async_copy(src, dst, ref.got.at[at]).start()
        pending[key] = (at, landed, left)

    done = set()

    def need(*keys):
        for key in keys:
            if key in done:
                continue
            done.add(key)
            at, landed, left = pending[key]
            for part in landed:
                pltpu.make_async_copy(part, part, ref.got.at[at]).wait()
            for part in left:
                pltpu.make_async_copy(part, part, ref.sent.at[at]).wait()

    barrier = pltpu.get_barrier_semaphore()
    greeted = [(y, (x + dx) % 4, (c + dc) % 2) for dx, dc in with_core]
    greeted += [((y + dy) % 4, x, (c + dc) % 2) for dy, dc in with_core[:-1]]
    for yy, xx, cc in greeted:
        pl.semaphore_signal(barrier, inc=1, device_id=device(yy, xx, cc), device_id_type=MESH)
    for array in (FIRST, SECOND, WEIGHT):
        begin((LOAD, array), (), [(ref.state_in[array], ref.final[array])], [ref.final[array]], ())
    for k in range(4):
        begin((LOAD, SMALL + k), (), [(ref.maps_in[k], ref.maps[k])], [ref.maps[k]], ())
    pl.semaphore_wait(barrier, len(greeted))

    def first(key, axis, src, dst):
        me = pl.ds(((x if axis == ALONG_X else y) * 2 + c) * 2, 2)
        sends = []
        for step, dc in with_core:
            cc = (c + dc) % 2
            if axis == ALONG_X:
                xx = (x + step) % 4
                sends.append((src.at[:, xx, cc], dst.at[me], device(y, xx, cc)))
            else:
                yy = (y + step) % 4
                sends.append((src.at[:, :, cc, yy], dst.at[me], device(yy, x, cc)))
        own = src.at[:, x, c] if axis == ALONG_X else src.at[:, :, c, y]
        begin(key, sends, [(own, dst.at[me])], [dst.at[pl.ds(0, 16)]], [dst.at[pl.ds(0, 14)]])

    def along(key, axis, src_of, dst):
        if axis == ALONG_X:
            sends = [(src_of((x + d) % 4), dst.at[x], device(y, (x + d) % 4, c)) for d in ring]
            own = [(src_of(x), dst.at[x])]
        else:
            sends = [(src_of((y + d) % 4), dst.at[y], device((y + d) % 4, x, c)) for d in ring]
            own = [(src_of(y), dst.at[y])]
        begin(key, sends, own, [dst], [dst.at[pl.ds(0, 3)]])

    def down(key, src_of, dst):
        sends = [(src_of((y + d) % 4), dst.at[:, y], device((y + d) % 4, x, c)) for d in ring]
        begin(key, sends, [(src_of(y), dst.at[:, y])], [dst], [dst.at[:, pl.ds(0, 3)]])

    def columns(stream, source):
        _, _, start, width = STREAMS[stream]
        return source if width == COLS else source.at[..., pl.ds(start, width)]

    def narrow(array):
        wide, thin = ref.final[array], ref.narrow[array - 1]
        need((LOAD, array))

        def body(at, carry):
            thin[at // 8, (at // 2) % 4, at % 2] = wide[at // 8, (at // 2) % 4, at % 2].astype(jnp.bfloat16)
            return carry

        lax.fori_loop(0, 16, body, 0)

    def state_first(stream):
        array, axis, _, _ = STREAMS[stream]
        source = ref.state_in[array] if array == WEIGHT else ref.narrow[array - 1]
        first((S1, stream), axis, columns(stream, source), ref.one[stream])

    def tables():
        need(*[(LOAD, SMALL + k) for k in range(4)])
        old, new, lost_ref, donor_ref = ref.maps
        lost = lost_ref[0]
        lost_half, lost_core = lost // 2, lost % 2

        def placed(relay, layer):
            there = old[relay, layer]
            twin = old[relay, jnp.maximum(layer - 1, 0)]
            return there, jnp.where((layer > 0) & (twin == there), 1, 0)

        held_at = [pick(x, [CANDIDATES[at][k] for at in range(4)]) for k in range(HELD)]
        for j in range(8):
            layer = 4 * (y % 2) + j
            donor = lost_ref[donor_ref[layer]]
            there, slot = placed(donor, layer)
            ref.pick[ALONG_X][j] = ((there % 4) * 2 + donor % 2) * 2 + slot
        for k in range(HELD):
            donor = lost_ref[donor_ref[held_at[k]]]
            there, slot = placed(donor, held_at[k])
            ref.pick[ALONG_Y][k] = (((donor // 2) * 2 + there // 4) * 2 + donor % 2) * 2 + slot
        for layer in range(LAYERS):
            donor = lost_ref[donor_ref[layer]]
            there = old[donor, layer]
            ref.src[ALONG_X][layer] = ((donor // 2) * 2 + there // 4) * 8 + layer - 4 * (there // 4)
            spots = [at * HELD + (CANDIDATES[at].index(layer) if layer in CANDIDATES[at] else 0) for at in range(4)]
            ref.src[ALONG_Y][layer] = pick(there % 4, spots)
        for k in range(HELD):
            for relay in range(4):
                there, slot = placed(relay, held_at[k])
                held = (there % 4 == x) & (lost != relay)
                from_y = (relay // 2) * 2 + there // 4
                ref.grad_at[k * 4 + relay] = jnp.where(held, (from_y * 2 + relay % 2) * 2 + slot, 16)
        for e in range(4):
            ref.lost_at[e] = ((lost_half * 2 + e // 2) * 2 + lost_core) * 2 + e % 2
        new_at = [new[layer] for layer in range(LAYERS)]
        inverse = [jnp.int32(LAYERS)] * 16
        for layer in range(LAYERS):
            there = new_at[layer]
            slot = jnp.int32(0)
            for before in range(layer):
                slot = slot + jnp.where(new_at[before] == there, 1, 0)
            ref.sum_at[layer] = (there % 4) * (HELD + 4) + HELD + (there // 4) * 2 + slot
            place = there * 2 + slot
            inverse = [jnp.where(place == at, layer, inverse[at]) for at in range(16)]
        for xx in range(4):
            for e in range(4):
                layer = inverse[((e // 2) * 4 + xx) * 2 + e % 2]
                ref.new_at[xx * 4 + e] = jnp.minimum(layer, LAYERS - 1)
                ref.new_has[xx * 4 + e] = jnp.where(layer < LAYERS, 1, 0)
        entries = {}
        for relay in range(4):
            for r in range(2):
                start = jnp.int32(0)
                for layer in range(LAYERS):
                    start = start + jnp.where(old[relay, layer] < r * 4 + x, 1, 0)
                for slot in range(2):
                    position = jnp.int32(0)
                    for k in range(HELD):
                        position = position + jnp.where(held_at[k] < start + slot, 1, 0)
                    entries[relay, r, slot] = jnp.minimum(position, HELD - 1)
        for yy in range(4):
            half, r = yy // 2, yy % 2
            here = lost_half == half
            for slot in range(2):
                even, odd = entries[half * 2, r, slot], entries[half * 2 + 1, r, slot]
                ref.mean_at[yy * 2 + slot] = jnp.where(here & (lost_core == 0), odd, even)
                ref.unit_at[yy * 2 + slot] = jnp.where(here, HELD + r * 2 + slot, odd)
        is_lost = lost == pipe
        count = jnp.int32(0)
        for layer in range(LAYERS):
            count = count + jnp.where(old[pipe, layer] == section, 1, 0)
        ref.flags[0] = jnp.where(is_lost, 1, 0)
        ref.flags[1] = jnp.where(is_lost | ((lost_half != pipe // 2) & (c == 1)), 1, 0)
        ref.flags[2] = jnp.where(is_lost | (count > 1), 1, 0)

    def grad_second():
        held, send = ref.grad_one, ref.grad_send
        held[16] = jnp.zeros((4, BAND, COLS), jnp.bfloat16)
        need((S1, GRADS))

        def merge(k, carry):
            total = held[ref.grad_at[k * 4]].astype(jnp.float32)
            for relay in range(1, 4):
                total = total + held[ref.grad_at[k * 4 + relay]].astype(jnp.float32)
            send[:, k] = total.astype(jnp.bfloat16)
            return carry

        lax.fori_loop(0, HELD, merge, 0)

        def keep(e, carry):
            send[:, HELD + e] = held[ref.lost_at[e]]
            return carry

        lax.fori_loop(0, 4, keep, 0)
        along((S2, GRADS), ALONG_X, lambda xx: send.at[xx], ref.grad_two)

    def means_back():
        got, mean, send = ref.grad_two, ref.mean, ref.mean_send
        need((S2, GRADS))
        for layer in range(LAYERS):
            at = ref.sum_at[layer]
            total = got[at // (HELD + 4), at % (HELD + 4)].astype(jnp.float32)
            for xx in range(4):
                if layer in CANDIDATES[xx]:
                    total = total + got[xx, CANDIDATES[xx].index(layer)].astype(jnp.float32)
            mean[layer] = total * 0.25
        for xx in range(4):
            for k in range(HELD):
                send[xx, k] = mean[CANDIDATES[xx][k]].astype(jnp.bfloat16)
        along((R1, MEANS), ALONG_X, lambda xx: send.at[xx], ref.mean_back)

    def state_second(stream):
        axis = STREAMS[stream][1]
        src, send, table = ref.one[stream], ref.two_send[stream], ref.pick[axis]
        need((S1, stream))

        def body(j, carry):
            send[:, j] = src[table[j]]
            return carry

        lax.fori_loop(0, send.shape[1], body, 0)
        along((S2, stream), 1 - axis, lambda at: send.at[at], ref.two[stream])

    def state_back(stream):
        array, axis, start, width = STREAMS[stream]
        src, send, mean = ref.two[stream], ref.back_send[stream], ref.mean
        held = src.shape[1]
        need((S2, stream))

        def body(i, carry):
            layer = ref.new_at[i]
            at = ref.src[axis][layer]
            value = src[at // held, at % held].astype(jnp.float32)
            grad = mean[layer] if width == COLS else mean[layer, :, start : start + width]
            if array == FIRST:
                value = BETA_ONE * value + (1.0 - BETA_ONE) * grad
            elif array == SECOND:
                value = BETA_TWO * value + (1.0 - BETA_TWO) * grad * grad
            send[i // 4, i % 4] = jnp.where(ref.new_has[i] == 1, value, 0.0).astype(jnp.bfloat16)
            return carry

        lax.fori_loop(0, 16, body, 0)
        along((R1, stream), ALONG_X, lambda xx: send.at[xx], ref.back[stream])

    def means_down():
        send, got = ref.mean_down, ref.mean_back
        need((R1, MEANS))
        for i in range(8):
            send[i // 2, :, i % 2] = got[:, ref.mean_at[i]]
        down((R2, MEANS), lambda yy: send.at[yy], ref.half_mean)

    def state_down(stream):
        array = STREAMS[stream][0]
        got, dst = ref.back[stream], columns(stream, ref.half[array])
        need((R1, stream))
        if array != FIRST:
            down((R2, stream), lambda yy: got.at[:, pl.ds((yy % 2) * 2, 2)], dst)
            return
        send, means = ref.pair_down, ref.mean_back
        for i in range(8):
            at = ref.unit_at[i]
            layer = means[:, jnp.minimum(at, HELD - 1)]
            send[i // 2, :, i % 2] = jnp.where(at < HELD, layer, got[:, jnp.maximum(at - HELD, 0)])
        down((R2, stream), lambda yy: send.at[yy], dst)

    def swap(key, src, dst):
        begin(key, [(src, dst.at[:, c], device(y, x, 1 - c))], [(src, dst.at[:, c])], [dst], [src])

    def swap_units(key, unit, src):
        need((R2, key))
        swap((R3, key), src, ref.units.at[unit])

    def survivors(slot):
        need((R3, MEANS), (R3, ONE), (LOAD, WEIGHT))
        w, one, two = ref.final
        lost, unit, second = ref.flags[0] == 1, ref.flags[1], ref.flags[2] == 1

        def body(i, carry):
            xb, cb, yb = i // 8, (i // 4) % 2, i % 4
            grad = ref.units[unit, xb, cb, yb, slot].astype(jnp.float32)
            next_one = BETA_ONE * one[slot, xb, cb, yb] + (1.0 - BETA_ONE) * grad
            next_two = BETA_TWO * two[slot, xb, cb, yb] + (1.0 - BETA_TWO) * grad * grad
            next_w = update(w[slot, xb, cb, yb].astype(jnp.float32), next_one, next_two)
            next_one = jnp.where(lost, grad, next_one)
            if slot == 1:
                next_one, next_two, next_w = [jnp.where(second, v, 0.0) for v in (next_one, next_two, next_w)]
            one[slot, xb, cb, yb] = next_one
            two[slot, xb, cb, yb] = next_two
            w[slot, xb, cb, yb] = next_w.astype(jnp.bfloat16)
            return carry

        lax.fori_loop(0, 32, body, 0, unroll=2)

    def lost_weights(stream):
        need((R2, W0), (R2, W1), (R2, ONE), (R2, stream))
        start, width = STREAMS[stream][2:]
        w, one, two = ref.half

        def body(i, carry):
            at = (i // 4, i % 4, slice(None), slice(None), slice(start, start + width))
            weight, next_one, next_two = [v[at].astype(jnp.float32) for v in (w, one, two)]
            w[at] = update(weight, next_one, next_two).astype(jnp.bfloat16)
            return carry

        lax.fori_loop(0, 16, body, 0)
        swap((R3, stream, SECOND), columns(stream, two), columns(stream, ref.lost_two))
        swap((R3, stream, WEIGHT), columns(stream, w), columns(stream, ref.lost_w))

    def lost_state(stream):
        need((R3, stream, SECOND), (R3, stream, WEIGHT))
        start, width = STREAMS[stream][2:]
        w, _, two = ref.final
        lost = ref.flags[0] == 1
        cols = slice(start, start + width)

        def body(i, carry):
            slot, xb, cb = i // 8, (i // 2) % 4, i % 2
            to, come = (slot, xb, cb, slice(None), slice(None), cols), (xb, cb, slice(None), slot, slice(None), cols)
            two[to] = jnp.where(lost, ref.lost_two[come].astype(jnp.float32), two[to])
            w[to] = jnp.where(lost, ref.lost_w[come], w[to])
            return carry

        lax.fori_loop(0, 16, body, 0)

    state_first(W0)
    first((S1, GRADS), ALONG_Y, ref.grads_in, ref.grad_one)
    narrow(FIRST)
    state_first(ONE)
    narrow(SECOND)
    state_first(TWO0)
    tables()
    state_second(W0)
    state_first(TWO1)
    grad_second()
    state_second(ONE)
    state_back(W0)
    means_back()
    state_first(W1)
    state_down(W0)
    state_back(ONE)
    state_second(TWO0)
    means_down()
    state_second(W1)
    state_down(ONE)
    state_back(W1)
    state_back(TWO0)
    state_second(TWO1)
    state_down(W1)
    state_down(TWO0)
    swap_units(MEANS, 0, ref.half_mean)
    swap_units(ONE, 1, ref.half[FIRST])
    state_back(TWO1)
    survivors(0)
    state_down(TWO1)
    survivors(1)
    lost_weights(TWO0)
    lost_weights(TWO1)
    lost_state(TWO0)
    lost_state(TWO1)
    need(*pending)


def exchange(grads, state, maps):
    bf16, f32, i32 = jnp.bfloat16, jnp.float32, jnp.int32
    hbm, vmem = pl.BlockSpec(memory_space=pltpu.HBM), pl.BlockSpec(memory_space=pltpu.VMEM)
    vm = lambda shape, dtype=bf16, width=COLS: pltpu.VMEM(shape + (BAND, width), dtype)
    table = lambda size: pltpu.SMEM((size,), i32)
    whole = (2, 4, 2, 4)
    streams = lambda shape_of: tuple(vm(shape_of(axis), bf16, width) for _, axis, _, width in STREAMS)
    second = lambda axis: (4, 8 if axis == ALONG_X else HELD)
    final = (vm(whole), vm(whole, f32), vm(whole, f32))
    buffers = Buffers(
        grads_in=hbm, state_in=(hbm,) * 3, maps_in=(hbm,) * 4, final=final,
        narrow=(vm(whole), vm(whole)),
        grad_one=vm((17, 4)), grad_send=vm((4, HELD + 4)), grad_two=vm((4, HELD + 4)), mean=vm((LAYERS,), f32),
        mean_send=vm((4, HELD)), mean_back=vm((4, HELD)), mean_down=vm((4, 4, 2)), pair_down=vm((4, 4, 2)),
        half_mean=vm((4, 4, 2)), half=(vm((4, 4, 2)),) * 3,
        units=vm((2, 4, 2, 4, 2)), lost_two=vm((4, 2, 4, 2)), lost_w=vm((4, 2, 4, 2)),
        one=streams(lambda axis: (16, 4)), two_send=streams(second), two=streams(second),
        back_send=streams(lambda axis: (4, 4)), back=streams(lambda axis: (4, 4)),
        maps=tuple(pltpu.SMEM(array.shape, i32) for array in maps),
        pick=(table(8), table(HELD)), src=(table(LAYERS), table(LAYERS)), grad_at=table(4 * HELD), lost_at=table(4),
        sum_at=table(LAYERS), new_at=table(16), new_has=table(16), mean_at=table(8), unit_at=table(8), flags=table(3),
        sent=pltpu.SemaphoreType.DMA((37,)), got=pltpu.SemaphoreType.DMA((37,)),
    )
    leaves, tree = jax.tree.flatten(buffers)
    in_hbm = lambda array: pltpu.with_memory_space_constraint(array, pltpu.HBM)
    return pl.pallas_call(
        lambda *refs: exchange_kernel(tree, *refs),
        out_shape=final,
        in_specs=[hbm] * 8,
        out_specs=(vmem,) * 3,
        scratch_shapes=leaves[11:],
        compiler_params=pltpu.CompilerParams(collective_id=0, has_side_effects=True, vmem_limit_bytes=28 << 20),
        name="exchange",
    )(*[in_hbm(array.reshape(whole + (BAND, COLS))) for array in (grads, *state)], *[in_hbm(array) for array in maps])


def store_kernel(*refs):
    copies = []
    for at in range(3):
        src, dst = refs[at], refs[3 + at]
        for slot in range(2):
            for half in range(2):
                rows = pl.ds(half * 2, 2)
                copies.append(pltpu.make_async_copy(src.at[slot, rows], dst.at[slot, rows], refs[6].at[len(copies)]))
                copies[-1].start()
    for copy in copies:
        copy.wait()


def store(arrays):
    vmem, hbm = pl.BlockSpec(memory_space=pltpu.VMEM), pl.BlockSpec(memory_space=pltpu.HBM)
    return pl.pallas_call(
        store_kernel,
        out_shape=tuple(pltpu.HBM(array.shape, array.dtype) for array in arrays),
        in_specs=[vmem] * 3,
        out_specs=(hbm,) * 3,
        scratch_shapes=[pltpu.SemaphoreType.DMA((12,))],
        compiler_params=pltpu.CompilerParams(vmem_limit_bytes=8 << 20),
        name="store",
    )(*[pltpu.with_memory_space_constraint(array, pltpu.VMEM) for array in arrays])


def per_device(weights, first_moment, second_moment, gradients, old_section, new_section, lost_pipe, donor_offset):
    shape = weights.shape
    state = (weights, first_moment, second_moment)
    final = exchange(gradients, state, (old_section, new_section, lost_pipe, donor_offset))
    return tuple(array.reshape(shape) for array in store(final))


def solution(mesh):
    big, small = P("pipe", "section", None, "tp", None), P()
    return jax.shard_map(
        per_device,
        mesh=mesh,
        in_specs=(big, big, big, big, small, small, small, small),
        out_specs=(big, big, big),
        check_vma=False,
    )
```

```python
from typing import Any, NamedTuple

import jax
import jax.numpy as jnp
from jax import lax
from jax.experimental import pallas as pl
from jax.experimental.pallas import tpu as pltpu
from jax.sharding import PartitionSpec as P

LEARN_RATE = 0.01
BETA_ONE = 0.9
BETA_TWO = 0.95
EPSILON = 1e-08
DECAY_RATE = 0.1
MESH = pl.DeviceIdType.MESH
LAYERS = 12
BAND = 16
COLS = 512

WEIGHT, FIRST, SECOND = range(3)
ALONG_X, ALONG_Y = range(2)
STREAMS = (
    (WEIGHT, ALONG_X, 0, 384),
    (WEIGHT, ALONG_X, 384, 128),
    (FIRST, ALONG_X, 0, 512),
    (SECOND, ALONG_Y, 0, 384),
    (SECOND, ALONG_Y, 384, 128),
)
W0, W1, ONE, TWO0, TWO1 = range(5)
S1, S2, R1, R2, R3, LOAD = range(6)
GRADS, MEANS, SMALL = range(10, 13)


def section_layers(section):
    last = section + min(section + 1, 4)
    return list(range(section + max(0, section - 4), last + 1))


CANDIDATES = [sorted(set(section_layers(x) + section_layers(x + 4))) for x in range(4)]
HELD = len(CANDIDATES[0])


class Buffers(NamedTuple):
    grads_in: Any
    state_in: Any
    maps_in: Any
    final: Any
    lost_two: Any
    lost_w: Any
    flags: Any
    narrow: Any
    grad_one: Any
    grad_send: Any
    grad_two: Any
    mean: Any
    mean_send: Any
    mean_back: Any
    mean_down: Any
    pair_down: Any
    units: Any
    half_w: Any
    half_two: Any
    far_w: Any
    far_two: Any
    one: Any
    two_send: Any
    two: Any
    back_send: Any
    back: Any
    maps: Any
    pick: Any
    src: Any
    grad_at: Any
    lost_at: Any
    sum_at: Any
    new_at: Any
    new_has: Any
    mean_at: Any
    unit_at: Any
    sent: Any
    got: Any


def pick(index, values):
    out = jnp.int32(values[0])
    for at in range(1, len(values)):
        out = jnp.where(index == at, jnp.int32(values[at]), out)
    return out


def update(weight, next_one, next_two):
    change = next_one / (jnp.sqrt(next_two) + EPSILON) + DECAY_RATE * weight
    return weight - LEARN_RATE * change


def exchange_kernel(tree, *refs):
    ref = jax.tree.unflatten(tree, refs)
    pipe, section, tp = lax.axis_index("pipe"), lax.axis_index("section"), lax.axis_index("tp")
    y = (pipe // 2) * 2 + section // 4
    x = section % 4
    c = pipe % 2
    ring = (1, 3, 2)
    with_core = [(step, dc) for step in ring for dc in (0, 1)] + [(0, 1)]
    pending = {}

    def device(yy, xx, cc):
        return ((yy // 2) * 2 + cc, (yy % 2) * 4 + xx, tp)

    def begin(key, sends, own, landed, left):
        at = len(pending)
        assert at < ref.sent.shape[0]
        for src, dst, target in sends:
            pltpu.make_async_remote_copy(
                src_ref=src, dst_ref=dst, send_sem=ref.sent.at[at], recv_sem=ref.got.at[at],
                device_id=target, device_id_type=MESH,
            ).start()
        for src, dst in own:
            pltpu.make_async_copy(src, dst, ref.got.at[at]).start()
        pending[key] = (at, landed, left)

    done = set()

    def need(*keys):
        for key in keys:
            if key in done:
                continue
            done.add(key)
            at, landed, left = pending[key]
            for part in landed:
                pltpu.make_async_copy(part, part, ref.got.at[at]).wait()
            for part in left:
                pltpu.make_async_copy(part, part, ref.sent.at[at]).wait()

    barrier = pltpu.get_barrier_semaphore()
    greeted = [(y, (x + dx) % 4, (c + dc) % 2) for dx, dc in with_core]
    greeted += [((y + dy) % 4, x, (c + dc) % 2) for dy, dc in with_core[:-1]]
    for yy, xx, cc in greeted:
        pl.semaphore_signal(barrier, inc=1, device_id=device(yy, xx, cc), device_id_type=MESH)
    for array in (FIRST, SECOND, WEIGHT):
        begin((LOAD, array), (), [(ref.state_in[array], ref.final[array])], [ref.final[array]], ())
    for k in range(4):
        begin((LOAD, SMALL + k), (), [(ref.maps_in[k], ref.maps[k])], [ref.maps[k]], ())
    pl.semaphore_wait(barrier, len(greeted))

    def first(key, axis, src, dst):
        me = pl.ds(((x if axis == ALONG_X else y) * 2 + c) * 2, 2)
        sends = []
        for step, dc in with_core:
            cc = (c + dc) % 2
            if axis == ALONG_X:
                xx = (x + step) % 4
                sends.append((src.at[:, xx, cc], dst.at[me], device(y, xx, cc)))
            else:
                yy = (y + step) % 4
                sends.append((src.at[:, :, cc, yy], dst.at[me], device(yy, x, cc)))
        own = src.at[:, x, c] if axis == ALONG_X else src.at[:, :, c, y]
        begin(key, sends, [(own, dst.at[me])], [dst.at[pl.ds(0, 16)]], [dst.at[pl.ds(0, 14)]])

    def along(key, axis, src_of, dst):
        if axis == ALONG_X:
            sends = [(src_of((x + d) % 4), dst.at[x], device(y, (x + d) % 4, c)) for d in ring]
            own = [(src_of(x), dst.at[x])]
        else:
            sends = [(src_of((y + d) % 4), dst.at[y], device((y + d) % 4, x, c)) for d in ring]
            own = [(src_of(y), dst.at[y])]
        begin(key, sends, own, [dst], [dst.at[pl.ds(0, 3)]])

    def down(key, src_of, dst):
        sends = [(src_of((y + d) % 4), dst.at[:, y], device((y + d) % 4, x, c)) for d in ring]
        begin(key, sends, [(src_of(y), dst.at[:, y])], [dst], [dst.at[:, pl.ds(0, 3)]])

    def columns(stream, source):
        _, _, start, width = STREAMS[stream]
        return source if width == COLS else source.at[..., pl.ds(start, width)]

    def narrow(array):
        wide, thin = ref.final[array], ref.narrow[array - 1]
        need((LOAD, array))

        def body(at, carry):
            thin[at // 8, (at // 2) % 4, at % 2] = wide[at // 8, (at // 2) % 4, at % 2].astype(jnp.bfloat16)
            return carry

        lax.fori_loop(0, 16, body, 0)

    def state_first(stream):
        array, axis, _, _ = STREAMS[stream]
        source = ref.state_in[array] if array == WEIGHT else ref.narrow[array - 1]
        first((S1, stream), axis, columns(stream, source), ref.one[stream])

    def tables():
        need(*[(LOAD, SMALL + k) for k in range(4)])
        old, new, lost_ref, donor_ref = ref.maps
        lost = lost_ref[0]
        lost_half, lost_core = lost // 2, lost % 2

        def placed(relay, layer):
            there = old[relay, layer]
            twin = old[relay, jnp.maximum(layer - 1, 0)]
            return there, jnp.where((layer > 0) & (twin == there), 1, 0)

        held_at = [pick(x, [CANDIDATES[at][k] for at in range(4)]) for k in range(HELD)]
        for j in range(8):
            layer = 4 * (y % 2) + j
            donor = lost_ref[donor_ref[layer]]
            there, slot = placed(donor, layer)
            ref.pick[ALONG_X][j] = ((there % 4) * 2 + donor % 2) * 2 + slot
        for k in range(HELD):
            donor = lost_ref[donor_ref[held_at[k]]]
            there, slot = placed(donor, held_at[k])
            ref.pick[ALONG_Y][k] = (((donor // 2) * 2 + there // 4) * 2 + donor % 2) * 2 + slot
        for layer in range(LAYERS):
            donor = lost_ref[donor_ref[layer]]
            there = old[donor, layer]
            ref.src[ALONG_X][layer] = ((donor // 2) * 2 + there // 4) * 8 + layer - 4 * (there // 4)
            spots = [at * HELD + (CANDIDATES[at].index(layer) if layer in CANDIDATES[at] else 0) for at in range(4)]
            ref.src[ALONG_Y][layer] = pick(there % 4, spots)
        for k in range(HELD):
            for relay in range(4):
                there, slot = placed(relay, held_at[k])
                held = (there % 4 == x) & (lost != relay)
                from_y = (relay // 2) * 2 + there // 4
                ref.grad_at[k * 4 + relay] = jnp.where(held, (from_y * 2 + relay % 2) * 2 + slot, 16)
        for e in range(4):
            ref.lost_at[e] = ((lost_half * 2 + e // 2) * 2 + lost_core) * 2 + e % 2
        new_at = [new[layer] for layer in range(LAYERS)]
        inverse = [jnp.int32(LAYERS)] * 16
        for layer in range(LAYERS):
            there = new_at[layer]
            slot = jnp.int32(0)
            for before in range(layer):
                slot = slot + jnp.where(new_at[before] == there, 1, 0)
            ref.sum_at[layer] = (there % 4) * (HELD + 4) + HELD + (there // 4) * 2 + slot
            place = there * 2 + slot
            inverse = [jnp.where(place == at, layer, inverse[at]) for at in range(16)]
        for xx in range(4):
            for e in range(4):
                layer = inverse[((e // 2) * 4 + xx) * 2 + e % 2]
                ref.new_at[xx * 4 + e] = jnp.minimum(layer, LAYERS - 1)
                ref.new_has[xx * 4 + e] = jnp.where(layer < LAYERS, 1, 0)
        entries = {}
        for relay in range(4):
            for r in range(2):
                start = jnp.int32(0)
                for layer in range(LAYERS):
                    start = start + jnp.where(old[relay, layer] < r * 4 + x, 1, 0)
                for slot in range(2):
                    position = jnp.int32(0)
                    for k in range(HELD):
                        position = position + jnp.where(held_at[k] < start + slot, 1, 0)
                    entries[relay, r, slot] = jnp.minimum(position, HELD - 1)
        for yy in range(4):
            half, r = yy // 2, yy % 2
            here = lost_half == half
            for slot in range(2):
                even, odd = entries[half * 2, r, slot], entries[half * 2 + 1, r, slot]
                ref.mean_at[yy * 2 + slot] = jnp.where(here & (lost_core == 0), odd, even)
                ref.unit_at[yy * 2 + slot] = jnp.where(here, HELD + r * 2 + slot, odd)
        is_lost = lost == pipe
        count = jnp.int32(0)
        for layer in range(LAYERS):
            count = count + jnp.where(old[pipe, layer] == section, 1, 0)
        ref.flags[0] = jnp.where(is_lost, 1, 0)
        ref.flags[1] = jnp.where(is_lost | ((lost_half != pipe // 2) & (c == 1)), 1, 0)
        ref.flags[2] = jnp.where(is_lost | (count > 1), 1, 0)

    def grad_second():
        held, send = ref.grad_one, ref.grad_send
        held[16] = jnp.zeros((4, BAND, COLS), jnp.bfloat16)
        need((S1, GRADS))

        def merge(k, carry):
            total = held[ref.grad_at[k * 4]].astype(jnp.float32)
            for relay in range(1, 4):
                total = total + held[ref.grad_at[k * 4 + relay]].astype(jnp.float32)
            send[:, k] = total.astype(jnp.bfloat16)
            return carry

        lax.fori_loop(0, HELD, merge, 0)

        def keep(e, carry):
            send[:, HELD + e] = held[ref.lost_at[e]]
            return carry

        lax.fori_loop(0, 4, keep, 0)
        along((S2, GRADS), ALONG_X, lambda xx: send.at[xx], ref.grad_two)

    def means_back():
        got, mean, send = ref.grad_two, ref.mean, ref.mean_send
        need((S2, GRADS))
        for layer in range(LAYERS):
            at = ref.sum_at[layer]
            total = got[at // (HELD + 4), at % (HELD + 4)].astype(jnp.float32)
            for xx in range(4):
                if layer in CANDIDATES[xx]:
                    total = total + got[xx, CANDIDATES[xx].index(layer)].astype(jnp.float32)
            mean[layer] = total * 0.25
        for xx in range(4):
            for k in range(HELD):
                send[xx, k] = mean[CANDIDATES[xx][k]].astype(jnp.bfloat16)
        along((R1, MEANS), ALONG_X, lambda xx: send.at[xx], ref.mean_back)

    def state_second(stream):
        axis = STREAMS[stream][1]
        src, send, table = ref.one[stream], ref.two_send[stream], ref.pick[axis]
        need((S1, stream))

        def body(j, carry):
            send[:, j] = src[table[j]]
            return carry

        lax.fori_loop(0, send.shape[1], body, 0)
        along((S2, stream), 1 - axis, lambda at: send.at[at], ref.two[stream])

    def state_back(stream):
        array, axis, start, width = STREAMS[stream]
        src, send, mean = ref.two[stream], ref.back_send[stream], ref.mean
        held = src.shape[1]
        need((S2, stream))

        def body(i, carry):
            layer = ref.new_at[i]
            at = ref.src[axis][layer]
            value = src[at // held, at % held].astype(jnp.float32)
            grad = mean[layer] if width == COLS else mean[layer, :, start : start + width]
            if array == FIRST:
                value = BETA_ONE * value + (1.0 - BETA_ONE) * grad
            elif array == SECOND:
                value = BETA_TWO * value + (1.0 - BETA_TWO) * grad * grad
            send[i // 4, i % 4] = jnp.where(ref.new_has[i] == 1, value, 0.0).astype(jnp.bfloat16)
            return carry

        lax.fori_loop(0, 16, body, 0)
        along((R1, stream), ALONG_X, lambda xx: send.at[xx], ref.back[stream])

    def means_down():
        send, got = ref.mean_down, ref.mean_back
        need((R1, MEANS))
        for i in range(8):
            send[i // 2, :, i % 2] = got[:, ref.mean_at[i]]
        down((R2, MEANS), lambda yy: send.at[yy], ref.units.at[0, :, c])

    def state_down(stream):
        array = STREAMS[stream][0]
        half = (ref.half_w, ref.units.at[1, :, c], ref.half_two)[array]
        got, dst = ref.back[stream], columns(stream, half)
        need((R1, stream))
        if array != FIRST:
            down((R2, stream), lambda yy: got.at[:, pl.ds((yy % 2) * 2, 2)], dst)
            return
        send, means = ref.pair_down, ref.mean_back
        for i in range(8):
            at = ref.unit_at[i]
            layer = means[:, jnp.minimum(at, HELD - 1)]
            send[i // 2, :, i % 2] = jnp.where(at < HELD, layer, got[:, jnp.maximum(at - HELD, 0)])
        down((R2, stream), lambda yy: send.at[yy], dst)

    def swap(key, src, dst, landed):
        begin(key, [(src, dst, device(y, x, 1 - c))], (), [landed], [src])

    def swap_units(key, unit):
        need((R2, key))
        mine, other = ref.units.at[unit, :, c], ref.units.at[unit, :, 1 - c]
        swap((R3, key), mine, mine, other)

    def survivors(slot):
        need((R3, MEANS), (R3, ONE), (LOAD, WEIGHT))
        w, one, two = ref.final
        lost, unit, second = ref.flags[0] == 1, ref.flags[1], ref.flags[2] == 1

        def body(i, carry):
            xb, cb, yb = i // 8, (i // 4) % 2, i % 4
            grad = ref.units[unit, xb, cb, yb, slot].astype(jnp.float32)
            next_one = BETA_ONE * one[slot, xb, cb, yb] + (1.0 - BETA_ONE) * grad
            next_two = BETA_TWO * two[slot, xb, cb, yb] + (1.0 - BETA_TWO) * grad * grad
            next_w = update(w[slot, xb, cb, yb].astype(jnp.float32), next_one, next_two)
            next_one = jnp.where(lost, grad, next_one)
            if slot == 1:
                next_one, next_two, next_w = [jnp.where(second, v, 0.0) for v in (next_one, next_two, next_w)]
            one[slot, xb, cb, yb] = next_one
            two[slot, xb, cb, yb] = next_two
            w[slot, xb, cb, yb] = next_w.astype(jnp.bfloat16)
            return carry

        lax.fori_loop(0, 32, body, 0, unroll=2)

    def swap_state(stream):
        need((R2, stream))
        src, dst = ((ref.half_w, ref.far_w) if STREAMS[stream][0] == WEIGHT else (ref.half_two, ref.far_two))
        far = columns(stream, dst)
        swap((R3, stream), columns(stream, src), far, far)

    def lost_rows(stream, w, two, core):
        start, width = STREAMS[stream][2:]
        cols = slice(start, start + width)

        def body(i, carry):
            at = (i // 4, i % 4, slice(None), slice(None), cols)
            weight, next_two = w[at].astype(jnp.float32), two[at].astype(jnp.float32)
            next_one = ref.units[1, i // 4, core, i % 4, :, :, cols].astype(jnp.float32)
            to = (slice(None), i // 4, core, i % 4, slice(None), cols)
            ref.lost_w[to] = update(weight, next_one, next_two).astype(jnp.bfloat16)
            ref.lost_two[to] = next_two
            return carry

        lax.fori_loop(0, 16, body, 0, unroll=2)

    def lost_own(stream):
        need((R2, W0), (R2, W1), (R2, ONE), (R2, stream))
        lost_rows(stream, ref.half_w, ref.half_two, c)

    def lost_far(stream):
        need((R3, W0), (R3, W1), (R3, ONE), (R3, stream))
        lost_rows(stream, ref.far_w, ref.far_two, 1 - c)

    first((S1, GRADS), ALONG_Y, ref.grads_in, ref.grad_one)
    state_first(W0)
    narrow(FIRST)
    state_first(ONE)
    narrow(SECOND)
    state_first(TWO0)
    tables()
    state_second(W0)
    state_first(TWO1)
    grad_second()
    state_second(ONE)
    state_back(W0)
    means_back()
    state_first(W1)
    state_down(W0)
    state_back(ONE)
    state_second(TWO0)
    means_down()
    state_second(W1)
    swap_state(W0)
    state_down(ONE)
    state_back(W1)
    state_back(TWO0)
    state_second(TWO1)
    state_down(W1)
    state_down(TWO0)
    swap_units(MEANS, 0)
    swap_units(ONE, 1)
    state_back(TWO1)
    survivors(0)
    swap_state(W1)
    state_down(TWO1)
    survivors(1)
    swap_state(TWO0)
    lost_own(TWO0)
    swap_state(TWO1)
    lost_own(TWO1)
    lost_far(TWO0)
    lost_far(TWO1)
    need(*pending)


def exchange(grads, state, maps):
    bf16, f32, i32 = jnp.bfloat16, jnp.float32, jnp.int32
    hbm, vmem = pl.BlockSpec(memory_space=pltpu.HBM), pl.BlockSpec(memory_space=pltpu.VMEM)
    vm = lambda shape, dtype=bf16, width=COLS: pltpu.VMEM(shape + (BAND, width), dtype)
    table = lambda size: pltpu.SMEM((size,), i32)
    whole = (2, 4, 2, 4)
    streams = lambda shape_of: tuple(vm(shape_of(axis), bf16, width) for _, axis, _, width in STREAMS)
    second = lambda axis: (4, 8 if axis == ALONG_X else HELD)
    final = (vm(whole), vm(whole, f32), vm(whole, f32))
    outputs = final + (vm(whole, f32), vm(whole), table(3))
    buffers = Buffers(
        grads_in=hbm, state_in=(hbm,) * 3, maps_in=(hbm,) * 4,
        final=final, lost_two=outputs[3], lost_w=outputs[4], flags=outputs[5],
        narrow=(vm(whole), vm(whole)),
        grad_one=vm((17, 4)), grad_send=vm((4, HELD + 4)), grad_two=vm((4, HELD + 4)), mean=vm((LAYERS,), f32),
        mean_send=vm((4, HELD)), mean_back=vm((4, HELD)), mean_down=vm((4, 4, 2)), pair_down=vm((4, 4, 2)),
        units=vm((2, 4, 2, 4, 2)), half_w=vm((4, 4, 2)), half_two=vm((4, 4, 2)), far_w=vm((4, 4, 2)), far_two=vm((4, 4, 2)),
        one=streams(lambda axis: (16, 4)), two_send=streams(second), two=streams(second),
        back_send=streams(lambda axis: (4, 4)), back=streams(lambda axis: (4, 4)),
        maps=tuple(pltpu.SMEM(array.shape, i32) for array in maps),
        pick=(table(8), table(HELD)), src=(table(LAYERS), table(LAYERS)), grad_at=table(4 * HELD), lost_at=table(4),
        sum_at=table(LAYERS), new_at=table(16), new_has=table(16), mean_at=table(8), unit_at=table(8),
        sent=pltpu.SemaphoreType.DMA((37,)), got=pltpu.SemaphoreType.DMA((37,)),
    )
    leaves, tree = jax.tree.flatten(buffers)
    in_hbm = lambda array: pltpu.with_memory_space_constraint(array, pltpu.HBM)
    return pl.pallas_call(
        lambda *refs: exchange_kernel(tree, *refs),
        out_shape=outputs[:5] + (jax.ShapeDtypeStruct((3,), i32),),
        in_specs=[hbm] * 8,
        out_specs=(vmem,) * 5 + (pl.BlockSpec(memory_space=pltpu.SMEM),),
        scratch_shapes=leaves[14:],
        compiler_params=pltpu.CompilerParams(collective_id=0, has_side_effects=True, vmem_limit_bytes=28 << 20),
        name="exchange",
    )(*[in_hbm(array.reshape(whole + (BAND, COLS))) for array in (grads, *state)], *[in_hbm(array) for array in maps])


def store_kernel(w, one, two, lost_two, lost_w, flags_in, out_w, out_one, out_two, flags, flag_sem, sem):
    load = pltpu.make_async_copy(flags_in, flags, flag_sem)
    load.start()

    def pieces(src, dst, at):
        copies = []
        for slot in range(2):
            for half in range(2):
                rows = pl.ds(half * 2, 2)
                copies.append(pltpu.make_async_copy(src.at[slot, rows], dst.at[slot, rows], sem.at[at + len(copies)]))
        return copies

    first = pieces(one, out_one, 0)
    for copy in first:
        copy.start()
    load.wait()
    held = pieces(two, out_two, 4) + pieces(w, out_w, 8)
    come = pieces(lost_two, out_two, 4) + pieces(lost_w, out_w, 8)

    @pl.when(flags[0] == 0)
    def _():
        for copy in held:
            copy.start()

    @pl.when(flags[0] == 1)
    def _():
        for copy in come:
            copy.start()

    for copy in first + held:
        copy.wait()


def store(arrays, flags):
    vmem, hbm = pl.BlockSpec(memory_space=pltpu.VMEM), pl.BlockSpec(memory_space=pltpu.HBM)
    return pl.pallas_call(
        store_kernel,
        out_shape=tuple(pltpu.HBM(array.shape, array.dtype) for array in arrays[:3]),
        in_specs=[vmem] * 5 + [pl.BlockSpec(memory_space=pl.ANY)],
        out_specs=(hbm,) * 3,
        scratch_shapes=[
            pltpu.SMEM(flags.shape, flags.dtype), pltpu.SemaphoreType.DMA, pltpu.SemaphoreType.DMA((12,)),
        ],
        compiler_params=pltpu.CompilerParams(vmem_limit_bytes=8 << 20),
        name="store",
    )(*[pltpu.with_memory_space_constraint(array, pltpu.VMEM) for array in arrays], flags)


def per_device(weights, first_moment, second_moment, gradients, old_section, new_section, lost_pipe, donor_offset):
    shape = weights.shape
    state = (weights, first_moment, second_moment)
    final = exchange(gradients, state, (old_section, new_section, lost_pipe, donor_offset))
    return tuple(array.reshape(shape) for array in store(final[:5], final[5]))


def solution(mesh):
    big, small = P("pipe", "section", None, "tp", None), P()
    return jax.shard_map(
        per_device,
        mesh=mesh,
        in_specs=(big, big, big, big, small, small, small, small),
        out_specs=(big, big, big),
        check_vma=False,
    )
```

```python
from typing import Any, NamedTuple

import jax
import jax.numpy as jnp
from jax import lax
from jax.experimental import pallas as pl
from jax.experimental.pallas import tpu as pltpu
from jax.sharding import PartitionSpec as P

LEARN_RATE = 0.01
BETA_ONE = 0.9
BETA_TWO = 0.95
EPSILON = 1e-08
DECAY_RATE = 0.1
MESH = pl.DeviceIdType.MESH
LAYERS = 12
BAND = 16
COLS = 512

WEIGHT, FIRST, SECOND = range(3)
ALONG_X, ALONG_Y = range(2)
STREAMS = (
    (WEIGHT, ALONG_X, 0, 384),
    (WEIGHT, ALONG_X, 384, 128),
    (FIRST, ALONG_X, 0, 512),
    (SECOND, ALONG_Y, 0, 384),
    (SECOND, ALONG_Y, 384, 128),
)
W0, W1, ONE, TWO0, TWO1 = range(5)
S1, S2, R1, R2, R3, LOAD = range(6)
GRADS, MEANS, SMALL = range(10, 13)


def section_layers(section):
    last = section + min(section + 1, 4)
    return list(range(section + max(0, section - 4), last + 1))


CANDIDATES = [sorted(set(section_layers(x) + section_layers(x + 4))) for x in range(4)]
HELD = len(CANDIDATES[0])


class Buffers(NamedTuple):
    grads_in: Any
    state_in: Any
    maps_in: Any
    final: Any
    lost_two: Any
    lost_w: Any
    flags: Any
    narrow: Any
    grad_one: Any
    grad_send: Any
    grad_two: Any
    mean: Any
    mean_send: Any
    mean_back: Any
    mean_down: Any
    pair_down: Any
    units: Any
    half_w: Any
    half_two: Any
    far_w: Any
    far_two: Any
    one: Any
    two_send: Any
    two: Any
    back_send: Any
    back: Any
    maps: Any
    pick: Any
    src: Any
    grad_at: Any
    lost_at: Any
    sum_at: Any
    new_at: Any
    new_has: Any
    mean_at: Any
    unit_at: Any
    sent: Any
    got: Any


def pick(index, values):
    out = jnp.int32(values[0])
    for at in range(1, len(values)):
        out = jnp.where(index == at, jnp.int32(values[at]), out)
    return out


def update(weight, next_one, next_two):
    change = next_one / (jnp.sqrt(next_two) + EPSILON) + DECAY_RATE * weight
    return weight - LEARN_RATE * change


def exchange_kernel(tree, *refs):
    ref = jax.tree.unflatten(tree, refs)
    pipe, section, tp = lax.axis_index("pipe"), lax.axis_index("section"), lax.axis_index("tp")
    y = (pipe // 2) * 2 + section // 4
    x = section % 4
    c = pipe % 2
    ring = (2, 1, 3)
    with_core = [(step, dc) for step in ring for dc in (0, 1)] + [(0, 1)]
    pending = {}

    def device(yy, xx, cc):
        return ((yy // 2) * 2 + cc, (yy % 2) * 4 + xx, tp)

    def begin(key, sends, own, landed, left):
        at = len(pending)
        assert at < ref.sent.shape[0]
        for src, dst, target in sends:
            pltpu.make_async_remote_copy(
                src_ref=src, dst_ref=dst, send_sem=ref.sent.at[at], recv_sem=ref.got.at[at],
                device_id=target, device_id_type=MESH,
            ).start()
        for src, dst in own:
            pltpu.make_async_copy(src, dst, ref.got.at[at]).start()
        pending[key] = (at, landed, left)

    done = set()

    def need(*keys):
        for key in keys:
            if key in done:
                continue
            done.add(key)
            at, landed, left = pending[key]
            for part in landed:
                pltpu.make_async_copy(part, part, ref.got.at[at]).wait()
            for part in left:
                pltpu.make_async_copy(part, part, ref.sent.at[at]).wait()

    barrier = pltpu.get_barrier_semaphore()
    greeted = [(y, (x + dx) % 4, (c + dc) % 2) for dx, dc in with_core]
    greeted += [((y + dy) % 4, x, (c + dc) % 2) for dy, dc in with_core[:-1]]
    for yy, xx, cc in greeted:
        pl.semaphore_signal(barrier, inc=1, device_id=device(yy, xx, cc), device_id_type=MESH)
    for array in (FIRST, SECOND, WEIGHT):
        begin((LOAD, array), (), [(ref.state_in[array], ref.final[array])], [ref.final[array]], ())
    for k in range(4):
        begin((LOAD, SMALL + k), (), [(ref.maps_in[k], ref.maps[k])], [ref.maps[k]], ())
    pl.semaphore_wait(barrier, len(greeted))

    def first(key, axis, src, dst):
        me = pl.ds(((x if axis == ALONG_X else y) * 2 + c) * 2, 2)
        sends = []
        for step, dc in with_core:
            cc = (c + dc) % 2
            if axis == ALONG_X:
                xx = (x + step) % 4
                sends.append((src.at[:, xx, cc], dst.at[me], device(y, xx, cc)))
            else:
                yy = (y + step) % 4
                sends.append((src.at[:, :, cc, yy], dst.at[me], device(yy, x, cc)))
        own = src.at[:, x, c] if axis == ALONG_X else src.at[:, :, c, y]
        begin(key, sends, [(own, dst.at[me])], [dst.at[pl.ds(0, 16)]], [dst.at[pl.ds(0, 14)]])

    def along(key, axis, src_of, dst):
        if axis == ALONG_X:
            sends = [(src_of((x + d) % 4), dst.at[x], device(y, (x + d) % 4, c)) for d in ring]
            own = [(src_of(x), dst.at[x])]
        else:
            sends = [(src_of((y + d) % 4), dst.at[y], device((y + d) % 4, x, c)) for d in ring]
            own = [(src_of(y), dst.at[y])]
        begin(key, sends, own, [dst], [dst.at[pl.ds(0, 3)]])

    def down(key, src_of, dst):
        sends = [(src_of((y + d) % 4), dst.at[:, y], device((y + d) % 4, x, c)) for d in ring]
        begin(key, sends, [(src_of(y), dst.at[:, y])], [dst], [dst.at[:, pl.ds(0, 3)]])

    def columns(stream, source):
        _, _, start, width = STREAMS[stream]
        return source if width == COLS else source.at[..., pl.ds(start, width)]

    def narrow(array):
        wide, thin = ref.final[array], ref.narrow[array - 1]
        need((LOAD, array))

        def body(at, carry):
            thin[at // 8, (at // 2) % 4, at % 2] = wide[at // 8, (at // 2) % 4, at % 2].astype(jnp.bfloat16)
            return carry

        lax.fori_loop(0, 16, body, 0)

    def state_first(stream):
        array, axis, _, _ = STREAMS[stream]
        source = ref.state_in[array] if array == WEIGHT else ref.narrow[array - 1]
        first((S1, stream), axis, columns(stream, source), ref.one[stream])

    def tables():
        need(*[(LOAD, SMALL + k) for k in range(4)])
        old, new, lost_ref, donor_ref = ref.maps
        lost = lost_ref[0]
        lost_half, lost_core = lost // 2, lost % 2

        def placed(relay, layer):
            there = old[relay, layer]
            twin = old[relay, jnp.maximum(layer - 1, 0)]
            return there, jnp.where((layer > 0) & (twin == there), 1, 0)

        held_at = [pick(x, [CANDIDATES[at][k] for at in range(4)]) for k in range(HELD)]
        for j in range(8):
            layer = 4 * (y % 2) + j
            donor = lost_ref[donor_ref[layer]]
            there, slot = placed(donor, layer)
            ref.pick[ALONG_X][j] = ((there % 4) * 2 + donor % 2) * 2 + slot
        for k in range(HELD):
            donor = lost_ref[donor_ref[held_at[k]]]
            there, slot = placed(donor, held_at[k])
            ref.pick[ALONG_Y][k] = (((donor // 2) * 2 + there // 4) * 2 + donor % 2) * 2 + slot
        for layer in range(LAYERS):
            donor = lost_ref[donor_ref[layer]]
            there = old[donor, layer]
            ref.src[ALONG_X][layer] = ((donor // 2) * 2 + there // 4) * 8 + layer - 4 * (there // 4)
            spots = [at * HELD + (CANDIDATES[at].index(layer) if layer in CANDIDATES[at] else 0) for at in range(4)]
            ref.src[ALONG_Y][layer] = pick(there % 4, spots)
        for k in range(HELD):
            for relay in range(4):
                there, slot = placed(relay, held_at[k])
                held = (there % 4 == x) & (lost != relay)
                from_y = (relay // 2) * 2 + there // 4
                ref.grad_at[k * 4 + relay] = jnp.where(held, (from_y * 2 + relay % 2) * 2 + slot, 16)
        for e in range(4):
            ref.lost_at[e] = ((lost_half * 2 + e // 2) * 2 + lost_core) * 2 + e % 2
        new_at = [new[layer] for layer in range(LAYERS)]
        inverse = [jnp.int32(LAYERS)] * 16
        for layer in range(LAYERS):
            there = new_at[layer]
            slot = jnp.int32(0)
            for before in range(layer):
                slot = slot + jnp.where(new_at[before] == there, 1, 0)
            ref.sum_at[layer] = (there % 4) * (HELD + 4) + HELD + (there // 4) * 2 + slot
            place = there * 2 + slot
            inverse = [jnp.where(place == at, layer, inverse[at]) for at in range(16)]
        for xx in range(4):
            for e in range(4):
                layer = inverse[((e // 2) * 4 + xx) * 2 + e % 2]
                ref.new_at[xx * 4 + e] = jnp.minimum(layer, LAYERS - 1)
                ref.new_has[xx * 4 + e] = jnp.where(layer < LAYERS, 1, 0)
        entries = {}
        for relay in range(4):
            for r in range(2):
                start = jnp.int32(0)
                for layer in range(LAYERS):
                    start = start + jnp.where(old[relay, layer] < r * 4 + x, 1, 0)
                for slot in range(2):
                    position = jnp.int32(0)
                    for k in range(HELD):
                        position = position + jnp.where(held_at[k] < start + slot, 1, 0)
                    entries[relay, r, slot] = jnp.minimum(position, HELD - 1)
        for yy in range(4):
            half, r = yy // 2, yy % 2
            here = lost_half == half
            for slot in range(2):
                even, odd = entries[half * 2, r, slot], entries[half * 2 + 1, r, slot]
                ref.mean_at[yy * 2 + slot] = jnp.where(here & (lost_core == 0), odd, even)
                ref.unit_at[yy * 2 + slot] = jnp.where(here, HELD + r * 2 + slot, odd)
        is_lost = lost == pipe
        count = jnp.int32(0)
        for layer in range(LAYERS):
            count = count + jnp.where(old[pipe, layer] == section, 1, 0)
        ref.flags[0] = jnp.where(is_lost, 1, 0)
        ref.flags[1] = jnp.where(is_lost | ((lost_half != pipe // 2) & (c == 1)), 1, 0)
        ref.flags[2] = jnp.where(is_lost | (count > 1), 1, 0)

    def grad_second():
        held, send = ref.grad_one, ref.grad_send
        held[16] = jnp.zeros((4, BAND, COLS), jnp.bfloat16)
        need((S1, GRADS))

        def merge(k, carry):
            total = held[ref.grad_at[k * 4]].astype(jnp.float32)
            for relay in range(1, 4):
                total = total + held[ref.grad_at[k * 4 + relay]].astype(jnp.float32)
            send[:, k] = total.astype(jnp.bfloat16)
            return carry

        lax.fori_loop(0, HELD, merge, 0)

        def keep(e, carry):
            send[:, HELD + e] = held[ref.lost_at[e]]
            return carry

        lax.fori_loop(0, 4, keep, 0)
        along((S2, GRADS), ALONG_X, lambda xx: send.at[xx], ref.grad_two)

    def means_back():
        got, mean, send = ref.grad_two, ref.mean, ref.mean_send
        need((S2, GRADS))
        for layer in range(LAYERS):
            at = ref.sum_at[layer]
            total = got[at // (HELD + 4), at % (HELD + 4)].astype(jnp.float32)
            for xx in range(4):
                if layer in CANDIDATES[xx]:
                    total = total + got[xx, CANDIDATES[xx].index(layer)].astype(jnp.float32)
            mean[layer] = total * 0.25
        for xx in range(4):
            for k in range(HELD):
                send[xx, k] = mean[CANDIDATES[xx][k]].astype(jnp.bfloat16)
        along((R1, MEANS), ALONG_X, lambda xx: send.at[xx], ref.mean_back)

    def state_second(stream):
        axis = STREAMS[stream][1]
        src, send, table = ref.one[stream], ref.two_send[stream], ref.pick[axis]
        need((S1, stream))

        def body(j, carry):
            send[:, j] = src[table[j]]
            return carry

        lax.fori_loop(0, send.shape[1], body, 0)
        along((S2, stream), 1 - axis, lambda at: send.at[at], ref.two[stream])

    def state_back(stream):
        array, axis, start, width = STREAMS[stream]
        src, send, mean = ref.two[stream], ref.back_send[stream], ref.mean
        held = src.shape[1]
        need((S2, stream))

        def body(i, carry):
            layer = ref.new_at[i]
            at = ref.src[axis][layer]
            value = src[at // held, at % held].astype(jnp.float32)
            grad = mean[layer] if width == COLS else mean[layer, :, start : start + width]
            if array == FIRST:
                value = BETA_ONE * value + (1.0 - BETA_ONE) * grad
            elif array == SECOND:
                value = BETA_TWO * value + (1.0 - BETA_TWO) * grad * grad
            send[i // 4, i % 4] = jnp.where(ref.new_has[i] == 1, value, 0.0).astype(jnp.bfloat16)
            return carry

        lax.fori_loop(0, 16, body, 0)
        along((R1, stream), ALONG_X, lambda xx: send.at[xx], ref.back[stream])

    def means_down():
        send, got = ref.mean_down, ref.mean_back
        need((R1, MEANS))
        for i in range(8):
            send[i // 2, :, i % 2] = got[:, ref.mean_at[i]]
        down((R2, MEANS), lambda yy: send.at[yy], ref.units.at[0, :, c])

    def state_down(stream):
        array = STREAMS[stream][0]
        half = (ref.half_w, ref.units.at[1, :, c], ref.half_two)[array]
        got, dst = ref.back[stream], columns(stream, half)
        need((R1, stream))
        if array != FIRST:
            down((R2, stream), lambda yy: got.at[:, pl.ds((yy % 2) * 2, 2)], dst)
            return
        send, means = ref.pair_down, ref.mean_back
        for i in range(8):
            at = ref.unit_at[i]
            layer = means[:, jnp.minimum(at, HELD - 1)]
            send[i // 2, :, i % 2] = jnp.where(at < HELD, layer, got[:, jnp.maximum(at - HELD, 0)])
        down((R2, stream), lambda yy: send.at[yy], dst)

    def swap(key, src, dst, landed):
        begin(key, [(src, dst, device(y, x, 1 - c))], (), [landed], [src])

    def swap_units(key, unit):
        need((R2, key))
        mine, other = ref.units.at[unit, :, c], ref.units.at[unit, :, 1 - c]
        swap((R3, key), mine, mine, other)

    def survivors(slot):
        need((R3, MEANS), (R3, ONE), (LOAD, WEIGHT))
        w, one, two = ref.final
        lost, unit, second = ref.flags[0] == 1, ref.flags[1], ref.flags[2] == 1

        def body(i, carry):
            xb, cb, yb = i // 8, (i // 4) % 2, i % 4
            grad = ref.units[unit, xb, cb, yb, slot].astype(jnp.float32)
            next_one = BETA_ONE * one[slot, xb, cb, yb] + (1.0 - BETA_ONE) * grad
            next_two = BETA_TWO * two[slot, xb, cb, yb] + (1.0 - BETA_TWO) * grad * grad
            next_w = update(w[slot, xb, cb, yb].astype(jnp.float32), next_one, next_two)
            next_one = jnp.where(lost, grad, next_one)
            if slot == 1:
                next_one, next_two, next_w = [jnp.where(second, v, 0.0) for v in (next_one, next_two, next_w)]
            one[slot, xb, cb, yb] = next_one
            two[slot, xb, cb, yb] = next_two
            w[slot, xb, cb, yb] = next_w.astype(jnp.bfloat16)
            return carry

        lax.fori_loop(0, 32, body, 0, unroll=2)

    def swap_state(stream):
        need((R2, stream))
        src, dst = ((ref.half_w, ref.far_w) if STREAMS[stream][0] == WEIGHT else (ref.half_two, ref.far_two))
        far = columns(stream, dst)
        swap((R3, stream), columns(stream, src), far, far)

    def lost_rows(stream, w, two, core):
        start, width = STREAMS[stream][2:]
        cols = slice(start, start + width)

        def body(i, carry):
            at = (i // 4, i % 4, slice(None), slice(None), cols)
            weight, next_two = w[at].astype(jnp.float32), two[at].astype(jnp.float32)
            next_one = ref.units[1, i // 4, core, i % 4, :, :, cols].astype(jnp.float32)
            to = (slice(None), i // 4, core, i % 4, slice(None), cols)
            ref.lost_w[to] = update(weight, next_one, next_two).astype(jnp.bfloat16)
            ref.lost_two[to] = next_two
            return carry

        lax.fori_loop(0, 16, body, 0, unroll=2)

    def lost_own(stream):
        need((R2, W0), (R2, W1), (R2, ONE), (R2, stream))
        lost_rows(stream, ref.half_w, ref.half_two, c)

    def lost_far(stream):
        need((R3, W0), (R3, W1), (R3, ONE), (R3, stream))
        lost_rows(stream, ref.far_w, ref.far_two, 1 - c)

    first((S1, GRADS), ALONG_Y, ref.grads_in, ref.grad_one)
    state_first(W0)
    narrow(FIRST)
    state_first(ONE)
    narrow(SECOND)
    state_first(TWO0)
    tables()
    state_second(W0)
    state_first(TWO1)
    grad_second()
    state_second(ONE)
    state_back(W0)
    means_back()
    state_first(W1)
    state_down(W0)
    state_back(ONE)
    state_second(TWO0)
    means_down()
    state_second(W1)
    swap_state(W0)
    state_down(ONE)
    state_back(W1)
    state_back(TWO0)
    state_second(TWO1)
    state_down(W1)
    state_down(TWO0)
    swap_units(MEANS, 0)
    swap_units(ONE, 1)
    state_back(TWO1)
    survivors(0)
    swap_state(W1)
    state_down(TWO1)
    survivors(1)
    swap_state(TWO0)
    lost_own(TWO0)
    swap_state(TWO1)
    lost_own(TWO1)
    lost_far(TWO0)
    lost_far(TWO1)
    need(*pending)


def exchange(grads, state, maps):
    bf16, f32, i32 = jnp.bfloat16, jnp.float32, jnp.int32
    hbm, vmem = pl.BlockSpec(memory_space=pltpu.HBM), pl.BlockSpec(memory_space=pltpu.VMEM)
    vm = lambda shape, dtype=bf16, width=COLS: pltpu.VMEM(shape + (BAND, width), dtype)
    table = lambda size: pltpu.SMEM((size,), i32)
    whole = (2, 4, 2, 4)
    streams = lambda shape_of: tuple(vm(shape_of(axis), bf16, width) for _, axis, _, width in STREAMS)
    second = lambda axis: (4, 8 if axis == ALONG_X else HELD)
    final = (vm(whole), vm(whole, f32), vm(whole, f32))
    outputs = final + (vm(whole, f32), vm(whole), table(3))
    buffers = Buffers(
        grads_in=hbm, state_in=(hbm,) * 3, maps_in=(hbm,) * 4,
        final=final, lost_two=outputs[3], lost_w=outputs[4], flags=outputs[5],
        narrow=(vm(whole), vm(whole)),
        grad_one=vm((17, 4)), grad_send=vm((4, HELD + 4)), grad_two=vm((4, HELD + 4)), mean=vm((LAYERS,), f32),
        mean_send=vm((4, HELD)), mean_back=vm((4, HELD)), mean_down=vm((4, 4, 2)), pair_down=vm((4, 4, 2)),
        units=vm((2, 4, 2, 4, 2)), half_w=vm((4, 4, 2)), half_two=vm((4, 4, 2)), far_w=vm((4, 4, 2)), far_two=vm((4, 4, 2)),
        one=streams(lambda axis: (16, 4)), two_send=streams(second), two=streams(second),
        back_send=streams(lambda axis: (4, 4)), back=streams(lambda axis: (4, 4)),
        maps=tuple(pltpu.SMEM(array.shape, i32) for array in maps),
        pick=(table(8), table(HELD)), src=(table(LAYERS), table(LAYERS)), grad_at=table(4 * HELD), lost_at=table(4),
        sum_at=table(LAYERS), new_at=table(16), new_has=table(16), mean_at=table(8), unit_at=table(8),
        sent=pltpu.SemaphoreType.DMA((37,)), got=pltpu.SemaphoreType.DMA((37,)),
    )
    leaves, tree = jax.tree.flatten(buffers)
    in_hbm = lambda array: pltpu.with_memory_space_constraint(array, pltpu.HBM)
    return pl.pallas_call(
        lambda *refs: exchange_kernel(tree, *refs),
        out_shape=outputs[:5] + (jax.ShapeDtypeStruct((3,), i32),),
        in_specs=[hbm] * 8,
        out_specs=(vmem,) * 5 + (pl.BlockSpec(memory_space=pltpu.SMEM),),
        scratch_shapes=leaves[14:],
        compiler_params=pltpu.CompilerParams(collective_id=0, has_side_effects=True, vmem_limit_bytes=28 << 20),
        name="exchange",
    )(*[in_hbm(array.reshape(whole + (BAND, COLS))) for array in (grads, *state)], *[in_hbm(array) for array in maps])


def store_kernel(w, one, two, lost_two, lost_w, flags_in, out_w, out_one, out_two, flags, flag_sem, sem):
    load = pltpu.make_async_copy(flags_in, flags, flag_sem)
    load.start()

    def pieces(src, dst, at):
        copies = []
        for slot in range(2):
            for quarter in range(4):
                rows = pl.ds(quarter, 1)
                copies.append(pltpu.make_async_copy(src.at[slot, rows], dst.at[slot, rows], sem.at[at + len(copies)]))
        return copies

    first = pieces(one, out_one, 0)
    for copy in first:
        copy.start()
    load.wait()
    held = pieces(two, out_two, 8) + pieces(w, out_w, 16)
    come = pieces(lost_two, out_two, 8) + pieces(lost_w, out_w, 16)

    @pl.when(flags[0] == 0)
    def _():
        for copy in held:
            copy.start()

    @pl.when(flags[0] == 1)
    def _():
        for copy in come:
            copy.start()

    for copy in first + held:
        copy.wait()


def store(arrays, flags):
    vmem, hbm = pl.BlockSpec(memory_space=pltpu.VMEM), pl.BlockSpec(memory_space=pltpu.HBM)
    return pl.pallas_call(
        store_kernel,
        out_shape=tuple(pltpu.HBM(array.shape, array.dtype) for array in arrays[:3]),
        in_specs=[vmem] * 5 + [pl.BlockSpec(memory_space=pl.ANY)],
        out_specs=(hbm,) * 3,
        scratch_shapes=[
            pltpu.SMEM(flags.shape, flags.dtype), pltpu.SemaphoreType.DMA, pltpu.SemaphoreType.DMA((24,)),
        ],
        compiler_params=pltpu.CompilerParams(vmem_limit_bytes=8 << 20),
        name="store",
    )(*[pltpu.with_memory_space_constraint(array, pltpu.VMEM) for array in arrays], flags)


def per_device(weights, first_moment, second_moment, gradients, old_section, new_section, lost_pipe, donor_offset):
    shape = weights.shape
    state = (weights, first_moment, second_moment)
    final = exchange(gradients, state, (old_section, new_section, lost_pipe, donor_offset))
    return tuple(array.reshape(shape) for array in store(final[:5], final[5]))


def solution(mesh):
    big, small = P("pipe", "section", None, "tp", None), P()
    return jax.shard_map(
        per_device,
        mesh=mesh,
        in_specs=(big, big, big, big, small, small, small, small),
        out_specs=(big, big, big),
        check_vma=False,
    )
```
